32 devices in a mesh: grp: 1, gx: 32 (over z, y, x, core), gy: 1.
Axes of the slice: x: 2, y: 2, z: 4, core: 2. Of those that a mesh axis runs over, the one named last changes fastest.
Arguments:
- incident: float32 [2, 16, 128, 128], P('grp', None, 'gx', 'gy'), may hold values from -6 to 6
- material: int32 [16, 128, 128], P('grp', 'gx', 'gy'), may hold values from 0 to 7
- contrast: float32 [8, 2], P('grp'), may hold values from 0.1 to 1.2
- w_first: bfloat16 [32, 4, 3, 3, 3], replicated, may hold values from -0.625 to 0.625
- w_middle: bfloat16 [32, 32, 3, 3, 3], replicated, may hold values from -0.21875 to 0.21875
- w_last: bfloat16 [2, 32, 3, 3, 3], replicated, may hold values from -0.21875 to 0.21875
- z_kernel: float32 [2, 16, 16], P('grp'), may hold values from -1 to 1
- spectral: float32 [2, 128, 128], P('grp', 'gx'), may hold values from -3 to 3
Outputs:
- total_field: float32 [2, 16, 128, 128], P('grp', None, 'gx', 'gy')
The draws below stay inside these ranges and needn't reach their ends.
Inputs may be any that keep to these rules, and one draw needn't show every extreme that they name: `material`: selects a row of contrast.
All inputs are finite; a program needn't handle non-finite values.
Results may differ from the reference program's by a relative error of at most 0.0013.
Values may be sent and summed in bfloat16 or wider, within the bound.
A program may use at most 64 MiB of HBM per device.

```python
import math
import jax
import jax.numpy as jnp
from jax import lax

NZ = 16
HID = 32
CLASSES = 8
ITERS = 1
NX = 128
NY = 128


def plant(values, key, smallest, largest):
    dims = values.shape
    place = [jax.random.randint(jax.random.fold_in(key, axis), (), 0, dims[axis]) for axis in range(len(dims))]
    values = values.at[tuple(place)].set(smallest)
    longest = dims.index(max(dims))
    place[longest] = (place[longest] + 1) % dims[longest]
    return values.at[tuple(place)].set(largest)


def steps_of(key, dims, pieces, least, top_value):
    gain, own = 1.0, jax.random.fold_in(key, 6)
    for dim, parts in pieces:
        heights = jnp.exp(jax.random.uniform(jax.random.fold_in(own, dim), (parts,), jnp.float32, least / len(pieces), top_value / len(pieces)))
        gain = gain * jnp.repeat(heights, dims[dim] // parts).reshape([-1 if axis == dim else 1 for axis in range(len(dims))])
    return gain


def gaussian(own_key, extent, scale, limit, pieces=(), kind=jnp.bfloat16):
    loudness = steps_of(own_key, extent, pieces, -0.22, 0.18) if pieces else 1.0
    values = jax.random.normal(own_key, extent, jnp.float32) * scale * loudness
    return jnp.minimum(jnp.maximum(values, -limit), limit).astype(kind)


def setup_inputs(seed: int = 0, part: int = 0) -> dict:
    splits = jax.random.split(jax.random.key(seed), 9)
    own_keys = jax.random.split(jax.random.fold_in(splits[8], part), 9)
    incident = gaussian(own_keys[0], (2, NZ, NX, NY), 1.0, 6.0, ((2, 32),), jnp.float32)
    material = plant(jax.random.randint(own_keys[1], (NZ, NX, NY), 0, CLASSES), jax.random.fold_in(own_keys[1], 1), 0, CLASSES - 1).astype(jnp.int32)
    contrast = jnp.clip(jax.random.uniform(own_keys[2], (CLASSES, 2), jnp.float32, 0.1, 1.2), 0.1, 1.2)
    w_first = gaussian(splits[3], (HID, 4, 3, 3, 3), 108 ** -0.5, 0.625)
    w_middle = gaussian(splits[4], (HID, HID, 3, 3, 3), (27 * HID) ** -0.5, 0.21875)
    w_last = gaussian(splits[5], (2, HID, 3, 3, 3), (27 * HID) ** -0.5, 0.21875)
    z_kernel = gaussian(own_keys[6], (2, NZ, NZ), (2 * NZ) ** -0.5, 1.0, (), jnp.float32)
    spectral = gaussian(own_keys[7], (2, NY, NX), 0.5, 3.0, ((1, 32),), jnp.float32)
    return dict(incident=incident, material=material, contrast=contrast, w_first=w_first, w_middle=w_middle, w_last=w_last, z_kernel=z_kernel, spectral=spectral)


def conv_layer(values, weights):
    return lax.conv_general_dilated(values[None], weights, (1, 1, 1), ((1, 1), (0, 0), (0, 0)), dimension_numbers=("NCDHW", "OIDHW", "NCDHW"), preferred_element_type=jnp.float32)[0]


def corrector_chain(padded, w_first, w_middle, w_last):
    hidden = jax.nn.gelu(conv_layer(padded, w_first), approximate=False).astype(jnp.bfloat16)
    hidden = jax.nn.gelu(conv_layer(hidden, w_middle), approximate=False).astype(jnp.bfloat16)
    return conv_layer(hidden, w_last)


def correction_field(features, w_first, w_middle, w_last):
    padded = jnp.pad(features, ((0, 0), (0, 0), (3, 3), (3, 3)), mode="wrap")
    block = math.gcd(NX, 64)
    count = NX // block

    def one_block(index):
        start = (index * block).astype(jnp.int32)
        piece = lax.dynamic_slice_in_dim(padded, start, block + 6, 2)
        return corrector_chain(piece, w_first, w_middle, w_last)

    result = lax.map(one_block, jnp.arange(count, dtype=jnp.int32))
    return jnp.moveaxis(result, 0, 2).reshape(2, NZ, NX, NY)


def green_apply(source, z_kernel, spectral):
    high = lax.Precision.HIGHEST
    kr, ki = z_kernel[0], z_kernel[1]
    lre = jnp.einsum("zw,wxy->zxy", kr, source[0], precision=high) - jnp.einsum("zw,wxy->zxy", ki, source[1], precision=high)
    lim = jnp.einsum("zw,wxy->zxy", kr, source[1], precision=high) + jnp.einsum("zw,wxy->zxy", ki, source[0], precision=high)
    spectrum = jnp.fft.fft2(lax.complex(lre, lim), axes=(1, 2))
    weight = jnp.transpose(lax.complex(spectral[0], spectral[1]))
    result = jnp.fft.ifft2(spectrum * weight[None], axes=(1, 2))
    return jnp.stack([jnp.real(result), jnp.imag(result)])


def reference(incident, material, contrast, w_first, w_middle, w_last, z_kernel, spectral):
    chi_re = contrast[:, 0][material]
    chi_im = contrast[:, 1][material]
    field = incident
    for step in range(ITERS):
        pol_re = chi_re * field[0] - chi_im * field[1]
        pol_im = chi_re * field[1] + chi_im * field[0]
        features = jnp.stack([field[0], field[1], pol_re, pol_im]).astype(jnp.bfloat16)
        source = jnp.stack([pol_re, pol_im]) + correction_field(features, w_first, w_middle, w_last)
        field = incident + green_apply(source, z_kernel, spectral)
    return field
```

```python
import functools
import math

import jax
import jax.numpy as jnp
import ml_dtypes
import numpy as np
from jax import lax
from jax.experimental import pallas as pl
from jax.experimental.pallas import tpu as pltpu
from jax.sharding import PartitionSpec as P


def padded_2(x, sides, width):
    for axis, dim in sides:
        count, length = (lax.axis_size(axis), x.shape[dim])
        up = [(i, (i + 1) % count) for i in range(count)]
        down = [(j, i) for i, j in up]
        last = lax.slice_in_dim(x, length - width, length, axis=dim)
        leading = lax.slice_in_dim(x, 0, width, axis=dim)
        before = lax.ppermute(last, axis, up)
        after = lax.ppermute(leading, axis, down)
        x = jnp.concatenate([before, x, after], axis=dim)
    return x


def conv_layer(values, weights):
    return lax.conv_general_dilated(
        values[None],
        weights,
        (1, 1, 1),
        ((1, 1), (0, 0), (0, 0)),
        dimension_numbers=("NCDHW", "OIDHW", "NCDHW"),
        preferred_element_type=jnp.float32,
    )[0]


def activate(values):
    return jax.nn.gelu(values, approximate=False).astype(jnp.bfloat16)


def dft_tables(length):
    positions = jnp.arange(length, dtype=jnp.int32)
    product = positions[:, None] * positions[None, :] % length
    angle = product.astype(jnp.float32) * (2.0 * math.pi / length)
    return (jnp.cos(angle), jnp.sin(angle))


def green_apply(source, z_kernel, spectral):
    high = lax.Precision.HIGHEST
    kr, ki = (z_kernel[0], z_kernel[1])
    lre = jnp.einsum("zw,wxy->zxy", kr, source[0], precision=high) - jnp.einsum(
        "zw,wxy->zxy", ki, source[1], precision=high
    )
    lim = jnp.einsum("zw,wxy->zxy", kr, source[1], precision=high) + jnp.einsum(
        "zw,wxy->zxy", ki, source[0], precision=high
    )
    columns = lax.all_to_all(jnp.stack([lre, lim]), "gy", split_axis=1, concat_axis=3, tiled=True)
    count_y = columns.shape[3]
    cos_y, sin_y = dft_tables(count_y)
    fwd_re = jnp.dot(columns[0], cos_y, precision=high) + jnp.dot(columns[1], sin_y, precision=high)
    fwd_im = jnp.dot(columns[1], cos_y, precision=high) - jnp.dot(columns[0], sin_y, precision=high)
    count_x = columns.shape[2] * lax.axis_size("gx")
    cos_x, sin_x = dft_tables(count_x)
    piece = lax.all_to_all(
        jnp.stack([fwd_re, fwd_im]), "gx", split_axis=3, concat_axis=2, tiled=True
    )
    ar = jnp.einsum("zxk,xq->zkq", piece[0], cos_x, precision=high) + jnp.einsum(
        "zxk,xq->zkq", piece[1], sin_x, precision=high
    )
    ai = jnp.einsum("zxk,xq->zkq", piece[1], cos_x, precision=high) - jnp.einsum(
        "zxk,xq->zkq", piece[0], sin_x, precision=high
    )
    br = spectral[0] * ar - spectral[1] * ai
    bi = spectral[0] * ai + spectral[1] * ar
    gr = jnp.einsum("zkq,qx->zxk", br, cos_x, precision=high) - jnp.einsum(
        "zkq,qx->zxk", bi, sin_x, precision=high
    )
    gi = jnp.einsum("zkq,qx->zxk", bi, cos_x, precision=high) + jnp.einsum(
        "zkq,qx->zxk", br, sin_x, precision=high
    )
    spread = jnp.stack([gr, gi]) / count_x
    rows = lax.all_to_all(spread, "gx", split_axis=2, concat_axis=3, tiled=True)
    inv_re = jnp.dot(rows[0], cos_y, precision=high) - jnp.dot(rows[1], sin_y, precision=high)
    inv_im = jnp.dot(rows[1], cos_y, precision=high) + jnp.dot(rows[0], sin_y, precision=high)
    scattered = jnp.stack([inv_re, inv_im]) / count_y
    return lax.all_to_all(scattered, "gy", split_axis=3, concat_axis=1, tiled=True)


def per_device(incident, material, contrast, w_first, w_middle, w_last, z_kernel, spectral):
    high = lax.Precision.HIGHEST
    classes = contrast.shape[0]
    selector = (material[None] == jnp.arange(classes, dtype=jnp.int32)[:, None, None, None]).astype(
        jnp.float32
    )
    chi_re = jnp.einsum("k,kzxy->zxy", contrast[:, 0], selector, precision=high)
    chi_im = jnp.einsum("k,kzxy->zxy", contrast[:, 1], selector, precision=high)
    field = incident
    pol_re = chi_re * field[0] - chi_im * field[1]
    pol_im = chi_re * field[1] + chi_im * field[0]
    features = jnp.stack([field[0], field[1], pol_re, pol_im]).astype(jnp.bfloat16)
    padded = padded_2(features, (("gx", 2), ("gy", 3)), 3)
    hidden = activate(conv_layer(padded, w_first))
    hidden = activate(conv_layer(hidden, w_middle))
    correction = conv_layer(hidden, w_last)
    source = jnp.stack([pol_re, pol_im]) + correction
    field = incident + green_apply(source, z_kernel, spectral)
    return field


def table_arrays(length, local):
    position = np.arange(length)
    angle = (position[:, None] * position[None, :] % length) * (2.0 * np.pi / length)
    cos, sin = np.cos(angle), np.sin(angle)
    order = position.reshape(length // local, local).T.reshape(-1)
    full = np.stack(
        [
            np.concatenate([cos, sin], axis=1),
            np.concatenate([cos[:, order], sin[:, order]], axis=1),
        ]
    ).astype(np.float32)
    high = full.astype(ml_dtypes.bfloat16)
    low = (full - high.astype(np.float32)).astype(ml_dtypes.bfloat16)
    return np.concatenate([high, low])


def split(x):
    high = x.astype(jnp.bfloat16)
    return high, (x - high.astype(jnp.float32)).astype(jnp.bfloat16)


def mxu(a, b):
    return jnp.dot(a, b, preferred_element_type=jnp.float32)


def dot3(a_high, a_low, b):
    b_high, b_low = split(b)
    return mxu(a_high, b_high) + (mxu(a_high, b_low) + mxu(a_low, b_high))


def gelu(x):
    return 0.5 * x * (1.0 + lax.erf(x * math.sqrt(0.5)))


def whole_kernel(
    dims,
    incident_ref,
    material_ref,
    contrast_ref,
    w1_ref,
    w2_ref,
    w3_ref,
    zk_ref,
    spectral_ref,
    tables_ref,
    out_ref,
    base1,
    base2,
    base3,
    wt1,
    wt2,
    wt3,
    own,
    halo_left,
    halo_right,
    pol,
    feat,
    h1,
    h2,
    o3,
    send_a,
    recv_a,
    send_b,
    recv_b,
    halo_send,
    halo_recv,
    a_send,
    a_recv,
    b_send,
    b_recv,
):
    n, nz, nx, ny, hid, classes = dims
    bf16, f32 = jnp.bfloat16, jnp.float32
    me = lax.axis_index("gx")
    right, left = lax.rem(me + 1, n), lax.rem(me + n - 1, n)
    mesh_id = pl.DeviceIdType.MESH

    barrier = pltpu.get_barrier_semaphore()

    def greet(k, carry):
        pl.semaphore_signal(
            barrier, inc=1, device_id={"gx": lax.rem(me + k, n)}, device_id_type=mesh_id
        )
        return carry

    lax.fori_loop(1, n, greet, 0)

    for x in range(nx):
        f0 = incident_ref[0, :, x, :]
        f1 = incident_ref[1, :, x, :]
        mat = material_ref[:, x, :]
        cr = jnp.zeros_like(f0)
        ci = jnp.zeros_like(f0)
        for k in range(classes):
            hit = mat == k
            cr = jnp.where(hit, contrast_ref[k, 0], cr)
            ci = jnp.where(hit, contrast_ref[k, 1], ci)
        pr = cr * f0 - ci * f1
        pi = cr * f1 + ci * f0
        pol[0, x] = pr
        pol[1, x] = pi
        own[x] = jnp.concatenate([f0, f1, pr, pi], axis=0).astype(bf16)

    pl.semaphore_wait(barrier, n - 1)

    to_right = pltpu.make_async_remote_copy(
        src_ref=own.at[pl.ds(nx - 3, 3)],
        dst_ref=halo_left,
        send_sem=halo_send.at[0],
        recv_sem=halo_recv.at[0],
        device_id={"gx": right},
        device_id_type=mesh_id,
    )
    to_left = pltpu.make_async_remote_copy(
        src_ref=own.at[pl.ds(0, 3)],
        dst_ref=halo_right,
        send_sem=halo_send.at[1],
        recv_sem=halo_recv.at[1],
        device_id={"gx": left},
        device_id_type=mesh_id,
    )
    to_right.start()
    to_left.start()

    base1[...] = jnp.zeros_like(base1)
    base2[...] = jnp.zeros_like(base2)
    base3[...] = jnp.zeros_like(base3)
    for a in range(3):
        for t in range(9):
            base1[t, :, a, 0:hid] = w1_ref[a * 9 + t].astype(f32)
            base2[t, :, hid * a : hid * a + hid] = w2_ref[a * 9 + t].astype(f32)
            b, d = divmod(t, 3)
            base3[b, 2 * d : 2 * d + 2, hid * a : hid * a + hid] = w3_ref[a * 9 + t].astype(f32)

    wide = jnp.transpose(base1[...].reshape(640, 128))[0:hid]
    lane = lax.broadcasted_iota(jnp.int32, wide.shape, 1) % nz
    for z in range(nz):
        block = wide if z == 1 else pltpu.roll(wide, (z - 1) % 640, 1)
        if z == 0:
            block = jnp.where(lane == nz - 1, 0.0, block)
        if z == nz - 1:
            block = jnp.where(lane == 0, 0.0, block)
        wt1[z * hid : z * hid + hid, :] = block.astype(bf16)
    for t in range(9):
        narrow = base2[t]
        for z in range(6):
            block = narrow if z == 0 else pltpu.roll(narrow, hid * z, 1)
            wt2[z * hid : z * hid + hid, t * 256 : t * 256 + 256] = block.astype(bf16)
    lane3 = lax.broadcasted_iota(jnp.int32, (8, 512), 1)
    for b in range(3):
        line = base3[b]
        rows = []
        for z in range(nz):
            block = line if z == 1 else pltpu.roll(line, (hid * (z - 1)) % 512, 1)
            if z == 0:
                block = jnp.where(lane3 >= 512 - hid, 0.0, block)
            if z == nz - 1:
                block = jnp.where(lane3 < hid, 0.0, block)
            rows.append(block)
        wt3[:, b * 512 : b * 512 + 512] = jnp.concatenate(rows, axis=0).astype(bf16)

    h1[:, :, 0:hid, :] = jnp.zeros((3, nx + 4, hid, ny), bf16)
    h1[:, :, (nz + 1) * hid :, :] = jnp.zeros((3, nx + 4, 3 * hid, ny), bf16)

    to_right.wait()
    to_left.wait()

    def shifted(x):
        return pltpu.roll(x, 1, 1), x, pltpu.roll(x, ny - 1, 1)

    for x in range(nx + 6):
        if x < 3:
            piece = halo_left[x]
        elif x < nx + 3:
            piece = own[x - 3]
        else:
            piece = halo_right[x - nx - 3]
        for d, moved in enumerate(shifted(piece.astype(f32))):
            feat[d, x] = moved.astype(bf16)

    def pair(ref, d, x, rows):
        return jnp.concatenate([ref[d, x, rows, :], ref[d, x + 1, rows, :]], axis=1)

    def first(i, carry):
        x = 2 * i
        parts = [pair(feat, d, x + b, slice(None)) for b in range(3) for d in range(3)]
        hidden = gelu(mxu(wt1[...], jnp.concatenate(parts + [parts[0]], axis=0)))
        for half in range(2):
            for d, moved in enumerate(shifted(hidden[:, half * ny : half * ny + ny])):
                h1[d, x + half, hid : (nz + 1) * hid, :] = moved.astype(bf16)
        return carry

    lax.fori_loop(0, (nx + 4) // 2, first, 0)

    def second(i, carry):
        x = 2 * (i // 3)
        start = pl.multiple_of((i % 3) * (6 * hid), 64)
        rows = pl.ds(start, 8 * hid)
        parts = [pair(h1, d, x + b, rows) for b in range(3) for d in range(3)]
        hidden = gelu(mxu(wt2[...], jnp.concatenate(parts, axis=0))).astype(bf16)
        for half in range(2):
            h2[x + half, pl.ds(start, 6 * hid), :] = hidden[:, half * ny : half * ny + ny]
        return carry

    lax.fori_loop(0, 3 * ((nx + 2) // 2), second, 0)

    for x in range(0, nx, 2):
        parts = [
            jnp.concatenate([h2[x + b, 0 : nz * hid, :], h2[x + b + 1, 0 : nz * hid, :]], axis=1)
            for b in range(3)
        ]
        taps = mxu(wt3[...], jnp.concatenate(parts, axis=0))
        for half in range(2):
            o3[x + half] = taps[:, half * ny : half * ny + ny].reshape(nz, 8, ny)

    sources = []
    for part in range(2):
        cells = []
        for x in range(nx):
            cells.append(
                pol[part, x]
                + (
                    pltpu.roll(o3[x, :, part, :], 1, 1)
                    + o3[x, :, 2 + part, :]
                    + pltpu.roll(o3[x, :, 4 + part, :], ny - 1, 1)
                )
            )
        sources.append(jnp.concatenate(cells, axis=1))
    zk_high, zk_low = split(zk_ref[...])
    both = [dot3(zk_high, zk_low, s) for s in sources]
    lre = both[0][0:nz] - both[1][nz:]
    lim = both[1][0:nz] + both[0][nz:]
    lifted = []
    for x in range(nx):
        lifted.append(lre[:, x * ny : x * ny + ny])
        lifted.append(lim[:, x * ny : x * ny + ny])
    lifted = jnp.transpose(jnp.concatenate(lifted, axis=0))

    lane = lax.broadcasted_iota(jnp.int32, (128, 128), 1)
    real = (lane // nz) % 2 == 0
    group = lax.broadcasted_iota(jnp.int32, (n, 128), 1) // (2 * nz)

    def swap(x):
        return jnp.where(real, pltpu.roll(x, 128 - nz, 1), -pltpu.roll(x, nz, 1))

    def transform(index, x, other):
        return dot3(tables_ref[index], tables_ref[index + 2], jnp.concatenate([x, other], axis=0))

    def regroup(ref):
        slabs = [ref[:, k, :] for k in range(4)]
        blocks = []
        for g in range(4):
            block = slabs[0] if g == 0 else pltpu.roll(slabs[0], (-32 * g) % 128, 1)
            for k in range(1, 4):
                moved = slabs[k] if k == g else pltpu.roll(slabs[k], (32 * (k - g)) % 128, 1)
                block = jnp.where(group == k, moved, block)
            blocks.append(block)
        return jnp.concatenate(blocks, axis=0)

    def exchange(value, send, recv, send_sem, recv_sem):
        for j in range(n):
            send[j] = value[4 * j : 4 * j + 4, :]
        recv[pl.ds(me, 1)] = send[pl.ds(me, 1)]

        def copy(target, slot):
            return pltpu.make_async_remote_copy(
                src_ref=send.at[target],
                dst_ref=recv.at[slot],
                send_sem=send_sem.at[target],
                recv_sem=recv_sem.at[slot],
                device_id={"gx": target},
                device_id_type=mesh_id,
            )

        def start(k, carry):
            copy(lax.rem(me + k, n), me).start()
            return carry

        def finish(k, carry):
            peer = lax.rem(me + n - k, n)
            copy(peer, peer).wait_recv()
            return carry

        def sent(k, carry):
            copy(lax.rem(me + k, n), me).wait_send()
            return carry

        lax.fori_loop(1, n, start, 0)
        lax.fori_loop(1, n, finish, 0)
        lax.fori_loop(1, n, sent, 0)

    exchange(transform(0, lifted, swap(lifted)), send_a, recv_a, a_send, a_recv)

    columns = regroup(recv_a)
    spectrum = transform(1, columns, swap(columns))
    weights = [
        jnp.transpose(
            jnp.concatenate(
                [
                    jnp.broadcast_to(spectral_ref[part, q : q + 1, :], (2 * nz, 128))
                    for q in range(4)
                ],
                axis=0,
            )
        )
        for part in range(2)
    ]
    scaled = weights[0] * spectrum - weights[1] * swap(spectrum)
    exchange(transform(0, scaled, -swap(scaled)), send_b, recv_b, b_send, b_recv)

    rows = regroup(recv_b)
    result = jnp.transpose(transform(1, rows, -swap(rows))) * (1.0 / (128 * 128))
    for x in range(nx):
        for part in range(2):
            first_row = (2 * x + part) * nz
            out_ref[part, :, x, :] = (
                incident_ref[part, :, x, :] + result[first_row : first_row + nz, :]
            )


def fused(mesh, incident, material, contrast, w_first, w_middle, w_last, z_kernel, spectral):
    n = mesh.shape["gx"]
    _, nz, nx, ny = incident.shape
    hid = w_middle.shape[0]
    f32, bf16 = jnp.float32, jnp.bfloat16
    w1 = jnp.transpose(w_first, (2, 3, 4, 1, 0)).reshape(27, 4, hid)
    w2 = jnp.transpose(w_middle, (2, 3, 4, 0, 1)).reshape(27, hid, hid)
    w3 = jnp.transpose(w_last, (2, 3, 4, 0, 1)).reshape(27, 2, hid)
    vmem = pl.BlockSpec(memory_space=pltpu.VMEM)
    smem = pl.BlockSpec(memory_space=pltpu.SMEM)
    dims = (n, nz, nx, ny, hid, contrast.shape[0])
    dma = pltpu.SemaphoreType.DMA
    return pl.pallas_call(
        functools.partial(whole_kernel, dims),
        out_shape=jax.ShapeDtypeStruct(incident.shape, f32),
        in_specs=[vmem, vmem, smem] + [vmem] * 6,
        out_specs=vmem,
        scratch_shapes=[
            pltpu.VMEM((10, 4, 16, 128), f32),
            pltpu.VMEM((9, hid, 256), f32),
            pltpu.VMEM((3, 8, 512), f32),
            pltpu.VMEM((nz * hid, 640), bf16),
            pltpu.VMEM((6 * hid, 9 * 256), bf16),
            pltpu.VMEM((nz * 8, 3 * 512), bf16),
            pltpu.VMEM((nx, 4 * nz, ny), bf16),
            pltpu.VMEM((3, 4 * nz, ny), bf16),
            pltpu.VMEM((3, 4 * nz, ny), bf16),
            pltpu.VMEM((2, nx, nz, ny), f32),
            pltpu.VMEM((3, nx + 6, 4 * nz, ny), bf16),
            pltpu.VMEM((3, nx + 4, (nz + 4) * hid, ny), bf16),
            pltpu.VMEM((nx + 2, (nz + 2) * hid, ny), bf16),
            pltpu.VMEM((nx, nz, 8, ny), f32),
            pltpu.VMEM((n, 4, 128), f32),
            pltpu.VMEM((n, 4, 128), f32),
            pltpu.VMEM((n, 4, 128), f32),
            pltpu.VMEM((n, 4, 128), f32),
            dma((2,)),
            dma((2,)),
            dma((n,)),
            dma((n,)),
            dma((n,)),
            dma((n,)),
        ],
        compiler_params=pltpu.CompilerParams(
            collective_id=0, has_side_effects=True, vmem_limit_bytes=40 << 20
        ),
    )(
        incident,
        material,
        contrast,
        w1,
        w2,
        w3,
        z_kernel.reshape(2 * nz, nz),
        spectral,
        jnp.asarray(table_arrays(128, nx)),
    )


def body(mesh, incident, material, contrast, w_first, w_middle, w_last, z_kernel, spectral):
    shapes_fit = (
        incident.shape == (2, 16, 4, 128)
        and mesh.shape["gx"] == 32
        and mesh.shape["gy"] == 1
        and w_middle.shape[0] == 32
    )
    args = (incident, material, contrast, w_first, w_middle, w_last, z_kernel, spectral)
    return fused(mesh, *args) if shapes_fit else per_device(*args)


def solution(mesh):
    placed = (
        P("grp", None, "gx", "gy"),
        P("grp", "gx", "gy"),
        P("grp", None),
        P(),
        P(),
        P(),
        P("grp", None, None),
        P("grp", "gx", None),
    )
    return jax.shard_map(
        functools.partial(body, mesh),
        mesh=mesh,
        in_specs=placed,
        out_specs=P("grp", None, "gx", "gy"),
        check_vma=False,
    )
```

```python
import functools
import math

import jax
import jax.numpy as jnp
import ml_dtypes
import numpy as np
from jax import lax
from jax.experimental import pallas as pl
from jax.experimental.pallas import tpu as pltpu
from jax.sharding import PartitionSpec as P


def padded_2(x, sides, width):
    for axis, dim in sides:
        count, length = (lax.axis_size(axis), x.shape[dim])
        up = [(i, (i + 1) % count) for i in range(count)]
        down = [(j, i) for i, j in up]
        last = lax.slice_in_dim(x, length - width, length, axis=dim)
        leading = lax.slice_in_dim(x, 0, width, axis=dim)
        before = lax.ppermute(last, axis, up)
        after = lax.ppermute(leading, axis, down)
        x = jnp.concatenate([before, x, after], axis=dim)
    return x


def conv_layer(values, weights):
    return lax.conv_general_dilated(
        values[None],
        weights,
        (1, 1, 1),
        ((1, 1), (0, 0), (0, 0)),
        dimension_numbers=("NCDHW", "OIDHW", "NCDHW"),
        preferred_element_type=jnp.float32,
    )[0]


def activate(values):
    return jax.nn.gelu(values, approximate=False).astype(jnp.bfloat16)


def dft_tables(length):
    positions = jnp.arange(length, dtype=jnp.int32)
    product = positions[:, None] * positions[None, :] % length
    angle = product.astype(jnp.float32) * (2.0 * math.pi / length)
    return (jnp.cos(angle), jnp.sin(angle))


def green_apply(source, z_kernel, spectral):
    high = lax.Precision.HIGHEST
    kr, ki = (z_kernel[0], z_kernel[1])
    lre = jnp.einsum("zw,wxy->zxy", kr, source[0], precision=high) - jnp.einsum(
        "zw,wxy->zxy", ki, source[1], precision=high
    )
    lim = jnp.einsum("zw,wxy->zxy", kr, source[1], precision=high) + jnp.einsum(
        "zw,wxy->zxy", ki, source[0], precision=high
    )
    columns = lax.all_to_all(jnp.stack([lre, lim]), "gy", split_axis=1, concat_axis=3, tiled=True)
    count_y = columns.shape[3]
    cos_y, sin_y = dft_tables(count_y)
    fwd_re = jnp.dot(columns[0], cos_y, precision=high) + jnp.dot(columns[1], sin_y, precision=high)
    fwd_im = jnp.dot(columns[1], cos_y, precision=high) - jnp.dot(columns[0], sin_y, precision=high)
    count_x = columns.shape[2] * lax.axis_size("gx")
    cos_x, sin_x = dft_tables(count_x)
    piece = lax.all_to_all(
        jnp.stack([fwd_re, fwd_im]), "gx", split_axis=3, concat_axis=2, tiled=True
    )
    ar = jnp.einsum("zxk,xq->zkq", piece[0], cos_x, precision=high) + jnp.einsum(
        "zxk,xq->zkq", piece[1], sin_x, precision=high
    )
    ai = jnp.einsum("zxk,xq->zkq", piece[1], cos_x, precision=high) - jnp.einsum(
        "zxk,xq->zkq", piece[0], sin_x, precision=high
    )
    br = spectral[0] * ar - spectral[1] * ai
    bi = spectral[0] * ai + spectral[1] * ar
    gr = jnp.einsum("zkq,qx->zxk", br, cos_x, precision=high) - jnp.einsum(
        "zkq,qx->zxk", bi, sin_x, precision=high
    )
    gi = jnp.einsum("zkq,qx->zxk", bi, cos_x, precision=high) + jnp.einsum(
        "zkq,qx->zxk", br, sin_x, precision=high
    )
    spread = jnp.stack([gr, gi]) / count_x
    rows = lax.all_to_all(spread, "gx", split_axis=2, concat_axis=3, tiled=True)
    inv_re = jnp.dot(rows[0], cos_y, precision=high) - jnp.dot(rows[1], sin_y, precision=high)
    inv_im = jnp.dot(rows[1], cos_y, precision=high) + jnp.dot(rows[0], sin_y, precision=high)
    scattered = jnp.stack([inv_re, inv_im]) / count_y
    return lax.all_to_all(scattered, "gy", split_axis=3, concat_axis=1, tiled=True)


def per_device(incident, material, contrast, w_first, w_middle, w_last, z_kernel, spectral):
    high = lax.Precision.HIGHEST
    classes = contrast.shape[0]
    selector = (material[None] == jnp.arange(classes, dtype=jnp.int32)[:, None, None, None]).astype(
        jnp.float32
    )
    chi_re = jnp.einsum("k,kzxy->zxy", contrast[:, 0], selector, precision=high)
    chi_im = jnp.einsum("k,kzxy->zxy", contrast[:, 1], selector, precision=high)
    field = incident
    pol_re = chi_re * field[0] - chi_im * field[1]
    pol_im = chi_re * field[1] + chi_im * field[0]
    features = jnp.stack([field[0], field[1], pol_re, pol_im]).astype(jnp.bfloat16)
    padded = padded_2(features, (("gx", 2), ("gy", 3)), 3)
    hidden = activate(conv_layer(padded, w_first))
    hidden = activate(conv_layer(hidden, w_middle))
    correction = conv_layer(hidden, w_last)
    source = jnp.stack([pol_re, pol_im]) + correction
    field = incident + green_apply(source, z_kernel, spectral)
    return field


def table_arrays(length, local):
    position = np.arange(length)
    angle = (position[:, None] * position[None, :] % length) * (2.0 * np.pi / length)
    cos, sin = np.cos(angle), np.sin(angle)
    order = position.reshape(length // local, local).T.reshape(-1)
    full = np.stack(
        [
            np.concatenate([cos, sin], axis=1),
            np.concatenate([cos[:, order], sin[:, order]], axis=1),
        ]
    ).astype(np.float32)
    high = full.astype(ml_dtypes.bfloat16)
    low = (full - high.astype(np.float32)).astype(ml_dtypes.bfloat16)
    return np.concatenate([high, low])


def split(x):
    high = x.astype(jnp.bfloat16)
    return high, (x - high.astype(jnp.float32)).astype(jnp.bfloat16)


def mxu(a, b):
    return jnp.dot(a, b, preferred_element_type=jnp.float32)


def dot3(a_high, a_low, b):
    b_high, b_low = split(b)
    return mxu(a_high, b_high) + (mxu(a_high, b_low) + mxu(a_low, b_high))


def gelu(x):
    return 0.5 * x * (1.0 + lax.erf(x * math.sqrt(0.5)))


def whole_kernel(
    dims,
    incident_hbm,
    material_hbm,
    contrast_hbm,
    w1_hbm,
    w2_hbm,
    w3_hbm,
    zk_hbm,
    spectral_hbm,
    tables_hbm,
    out_ref,
    incident_ref,
    material_ref,
    contrast_ref,
    w1_ref,
    w2_ref,
    w3_ref,
    zk_ref,
    spectral_ref,
    tables_ref,
    load_sem,
    base1,
    base2,
    base3,
    wt1,
    wt2,
    wt3,
    own,
    halo_left,
    halo_right,
    pol,
    feat,
    h1,
    h2,
    o3,
    send_a,
    recv_a,
    send_b,
    recv_b,
    halo_send,
    halo_recv,
    a_send,
    a_recv,
    b_send,
    b_recv,
):
    n, nz, nx, ny, hid, classes = dims
    bf16, f32 = jnp.bfloat16, jnp.float32
    me = lax.axis_index("gx")
    right, left = lax.rem(me + 1, n), lax.rem(me + n - 1, n)
    mesh_id = pl.DeviceIdType.MESH

    pairs = (
        (incident_hbm, incident_ref),
        (material_hbm, material_ref),
        (contrast_hbm, contrast_ref),
        (w1_hbm, w1_ref),
        (w2_hbm, w2_ref),
        (w3_hbm, w3_ref),
        (zk_hbm, zk_ref),
        (spectral_hbm, spectral_ref),
        (tables_hbm, tables_ref),
    )
    loads = [
        pltpu.make_async_copy(src, dst, load_sem.at[k]) for k, (src, dst) in enumerate(pairs)
    ]
    for load in loads:
        load.start()

    barrier = pltpu.get_barrier_semaphore()

    def greet(k, carry):
        pl.semaphore_signal(
            barrier, inc=1, device_id={"gx": lax.rem(me + k, n)}, device_id_type=mesh_id
        )
        return carry

    lax.fori_loop(1, n, greet, 0, unroll=True)

    for load in loads[:3]:
        load.wait()

    for x in range(nx):
        f0 = incident_ref[0, :, x, :]
        f1 = incident_ref[1, :, x, :]
        mat = material_ref[:, x, :]
        cr = jnp.zeros_like(f0)
        ci = jnp.zeros_like(f0)
        for k in range(classes):
            hit = mat == k
            cr = jnp.where(hit, contrast_ref[0:1, k : k + 1], cr)
            ci = jnp.where(hit, contrast_ref[1:2, k : k + 1], ci)
        pr = cr * f0 - ci * f1
        pi = cr * f1 + ci * f0
        pol[0, x] = pr
        pol[1, x] = pi
        own[x] = jnp.concatenate([f0, f1, pr, pi], axis=0).astype(bf16)

    pl.semaphore_wait(barrier, n - 1)

    to_right = pltpu.make_async_remote_copy(
        src_ref=own.at[pl.ds(nx - 3, 3)],
        dst_ref=halo_left,
        send_sem=halo_send.at[0],
        recv_sem=halo_recv.at[0],
        device_id={"gx": right},
        device_id_type=mesh_id,
    )
    to_left = pltpu.make_async_remote_copy(
        src_ref=own.at[pl.ds(0, 3)],
        dst_ref=halo_right,
        send_sem=halo_send.at[1],
        recv_sem=halo_recv.at[1],
        device_id={"gx": left},
        device_id_type=mesh_id,
    )
    to_right.start()
    to_left.start()

    for load in loads[3:]:
        load.wait()
    base1[...] = jnp.zeros_like(base1)
    base2[...] = jnp.zeros_like(base2)
    base3[...] = jnp.zeros_like(base3)
    for a in range(3):
        for t in range(9):
            base1[t, :, a, 0:hid] = w1_ref[a * 9 + t].astype(f32)
            base2[t, :, hid * a : hid * a + hid] = w2_ref[a * 9 + t].astype(f32)
            b, d = divmod(t, 3)
            base3[b, 2 * d : 2 * d + 2, hid * a : hid * a + hid] = w3_ref[a * 9 + t].astype(f32)

    wide = jnp.transpose(base1[...].reshape(640, 128))[0:hid]
    lane = lax.broadcasted_iota(jnp.int32, wide.shape, 1) % nz
    for z in range(nz):
        block = wide if z == 1 else pltpu.roll(wide, (z - 1) % 640, 1)
        if z == 0:
            block = jnp.where(lane == nz - 1, 0.0, block)
        if z == nz - 1:
            block = jnp.where(lane == 0, 0.0, block)
        wt1[z * hid : z * hid + hid, :] = block.astype(bf16)
    for t in range(9):
        narrow = base2[t]
        for z in range(6):
            block = narrow if z == 0 else pltpu.roll(narrow, hid * z, 1)
            wt2[z * hid : z * hid + hid, t * 256 : t * 256 + 256] = block.astype(bf16)
    lane3 = lax.broadcasted_iota(jnp.int32, (8, 512), 1)
    for b in range(3):
        line = base3[b]
        rows = []
        for z in range(nz):
            block = line if z == 1 else pltpu.roll(line, (hid * (z - 1)) % 512, 1)
            if z == 0:
                block = jnp.where(lane3 >= 512 - hid, 0.0, block)
            if z == nz - 1:
                block = jnp.where(lane3 < hid, 0.0, block)
            rows.append(block)
        wt3[:, b * 512 : b * 512 + 512] = jnp.concatenate(rows, axis=0).astype(bf16)

    h1[:, :, 0:hid, :] = jnp.zeros((3, nx + 4, hid, ny), bf16)
    h1[:, :, (nz + 1) * hid :, :] = jnp.zeros((3, nx + 4, 3 * hid, ny), bf16)

    to_right.wait()
    to_left.wait()

    def shifted(x):
        return pltpu.roll(x, 1, 1), x, pltpu.roll(x, ny - 1, 1)

    for x in range(nx + 6):
        if x < 3:
            piece = halo_left[x]
        elif x < nx + 3:
            piece = own[x - 3]
        else:
            piece = halo_right[x - nx - 3]
        for d, moved in enumerate(shifted(piece.astype(f32))):
            feat[d, x] = moved.astype(bf16)

    def pair(ref, d, x, rows):
        return jnp.concatenate([ref[d, x, rows, :], ref[d, x + 1, rows, :]], axis=1)

    def first(i, carry):
        x = 2 * i
        parts = [pair(feat, d, x + b, slice(None)) for b in range(3) for d in range(3)]
        hidden = gelu(mxu(wt1[...], jnp.concatenate(parts + [parts[0]], axis=0)))
        for half in range(2):
            for d, moved in enumerate(shifted(hidden[:, half * ny : half * ny + ny])):
                h1[d, x + half, hid : (nz + 1) * hid, :] = moved.astype(bf16)
        return carry

    lax.fori_loop(0, (nx + 4) // 2, first, 0)

    def second(i, carry):
        x = 2 * (i // 3)
        start = pl.multiple_of((i % 3) * (6 * hid), 64)
        rows = pl.ds(start, 8 * hid)
        parts = [pair(h1, d, x + b, rows) for b in range(3) for d in range(3)]
        hidden = gelu(mxu(wt2[...], jnp.concatenate(parts, axis=0))).astype(bf16)
        for half in range(2):
            h2[x + half, pl.ds(start, 6 * hid), :] = hidden[:, half * ny : half * ny + ny]
        return carry

    lax.fori_loop(0, 3 * ((nx + 2) // 2), second, 0)

    for x in range(0, nx, 2):
        parts = [
            jnp.concatenate([h2[x + b, 0 : nz * hid, :], h2[x + b + 1, 0 : nz * hid, :]], axis=1)
            for b in range(3)
        ]
        taps = mxu(wt3[...], jnp.concatenate(parts, axis=0))
        for half in range(2):
            o3[x + half] = taps[:, half * ny : half * ny + ny].reshape(nz, 8, ny)

    sources = []
    for part in range(2):
        cells = []
        for x in range(nx):
            cells.append(
                pol[part, x]
                + (
                    pltpu.roll(o3[x, :, part, :], 1, 1)
                    + o3[x, :, 2 + part, :]
                    + pltpu.roll(o3[x, :, 4 + part, :], ny - 1, 1)
                )
            )
        sources.append(jnp.concatenate(cells, axis=1))
    zk_high, zk_low = split(zk_ref[...])
    both = [dot3(zk_high, zk_low, s) for s in sources]
    lre = both[0][0:nz] - both[1][nz:]
    lim = both[1][0:nz] + both[0][nz:]
    lifted = []
    for x in range(nx):
        lifted.append(lre[:, x * ny : x * ny + ny])
        lifted.append(lim[:, x * ny : x * ny + ny])
    lifted = jnp.transpose(jnp.concatenate(lifted, axis=0))

    lane = lax.broadcasted_iota(jnp.int32, (128, 128), 1)
    real = (lane // nz) % 2 == 0
    group = lax.broadcasted_iota(jnp.int32, (n, 128), 1) // (2 * nz)

    def swap(x):
        return jnp.where(real, pltpu.roll(x, 128 - nz, 1), -pltpu.roll(x, nz, 1))

    def transform(index, x, other):
        return dot3(tables_ref[index], tables_ref[index + 2], jnp.concatenate([x, other], axis=0))

    def regroup(ref):
        slabs = [ref[:, k, :] for k in range(4)]
        blocks = []
        for g in range(4):
            block = slabs[0] if g == 0 else pltpu.roll(slabs[0], (-32 * g) % 128, 1)
            for k in range(1, 4):
                moved = slabs[k] if k == g else pltpu.roll(slabs[k], (32 * (k - g)) % 128, 1)
                block = jnp.where(group == k, moved, block)
            blocks.append(block)
        return jnp.concatenate(blocks, axis=0)

    def exchange(value, send, recv, send_sem, recv_sem):
        for j in range(n):
            send[j] = value[4 * j : 4 * j + 4, :]
        recv[pl.ds(me, 1)] = send[pl.ds(me, 1)]

        def start(k, carry):
            target = lax.rem(me + k, n)
            pltpu.make_async_remote_copy(
                src_ref=send.at[target],
                dst_ref=recv.at[me],
                send_sem=send_sem,
                recv_sem=recv_sem,
                device_id={"gx": target},
                device_id_type=mesh_id,
            ).start()
            return carry

        lax.fori_loop(1, n, start, 0, unroll=True)
        wait_all(recv, recv_sem)

    def wait_all(ref, sem):
        pltpu.make_async_copy(ref.at[pl.ds(0, n - 1)], ref.at[pl.ds(0, n - 1)], sem).wait()

    exchange(transform(0, lifted, swap(lifted)), send_a, recv_a, a_send, a_recv)

    columns = regroup(recv_a)
    spectrum = transform(1, columns, swap(columns))
    weights = [
        jnp.transpose(
            jnp.concatenate(
                [
                    jnp.broadcast_to(spectral_ref[part, q : q + 1, :], (2 * nz, 128))
                    for q in range(4)
                ],
                axis=0,
            )
        )
        for part in range(2)
    ]
    scaled = weights[0] * spectrum - weights[1] * swap(spectrum)
    exchange(transform(0, scaled, -swap(scaled)), send_b, recv_b, b_send, b_recv)

    rows = regroup(recv_b)
    result = jnp.transpose(transform(1, rows, -swap(rows))) * (1.0 / (128 * 128))
    for x in range(nx):
        for part in range(2):
            first_row = (2 * x + part) * nz
            out_ref[part, :, x, :] = (
                incident_ref[part, :, x, :] + result[first_row : first_row + nz, :]
            )
    wait_all(send_a, a_send)
    wait_all(send_b, b_send)


def fused(mesh, incident, material, contrast, w_first, w_middle, w_last, z_kernel, spectral):
    n = mesh.shape["gx"]
    _, nz, nx, ny = incident.shape
    hid = w_middle.shape[0]
    f32, bf16 = jnp.float32, jnp.bfloat16
    w1 = jnp.transpose(w_first, (2, 3, 4, 1, 0)).reshape(27, 4, hid)
    w2 = jnp.transpose(w_middle, (2, 3, 4, 0, 1)).reshape(27, hid, hid)
    w3 = jnp.transpose(w_last, (2, 3, 4, 0, 1)).reshape(27, 2, hid)
    vmem = pl.BlockSpec(memory_space=pltpu.VMEM)
    hbm = pl.BlockSpec(memory_space=pltpu.HBM)
    dims = (n, nz, nx, ny, hid, contrast.shape[0])
    dma = pltpu.SemaphoreType.DMA
    operands = (
        incident,
        material,
        contrast.T,
        w1,
        w2,
        w3,
        z_kernel.reshape(2 * nz, nz),
        spectral,
        jnp.asarray(table_arrays(128, nx)),
    )
    return pl.pallas_call(
        functools.partial(whole_kernel, dims),
        out_shape=jax.ShapeDtypeStruct(incident.shape, f32),
        in_specs=[hbm] * len(operands),
        out_specs=vmem,
        scratch_shapes=[pltpu.VMEM(x.shape, x.dtype) for x in operands]
        + [
            dma((len(operands),)),
            pltpu.VMEM((10, 4, 16, 128), f32),
            pltpu.VMEM((9, hid, 256), f32),
            pltpu.VMEM((3, 8, 512), f32),
            pltpu.VMEM((nz * hid, 640), bf16),
            pltpu.VMEM((6 * hid, 9 * 256), bf16),
            pltpu.VMEM((nz * 8, 3 * 512), bf16),
            pltpu.VMEM((nx, 4 * nz, ny), bf16),
            pltpu.VMEM((3, 4 * nz, ny), bf16),
            pltpu.VMEM((3, 4 * nz, ny), bf16),
            pltpu.VMEM((2, nx, nz, ny), f32),
            pltpu.VMEM((3, nx + 6, 4 * nz, ny), bf16),
            pltpu.VMEM((3, nx + 4, (nz + 4) * hid, ny), bf16),
            pltpu.VMEM((nx + 2, (nz + 2) * hid, ny), bf16),
            pltpu.VMEM((nx, nz, 8, ny), f32),
            pltpu.VMEM((n, 4, 128), f32),
            pltpu.VMEM((n, 4, 128), f32),
            pltpu.VMEM((n, 4, 128), f32),
            pltpu.VMEM((n, 4, 128), f32),
            dma((2,)),
            dma((2,)),
            dma,
            dma,
            dma,
            dma,
        ],
        compiler_params=pltpu.CompilerParams(
            collective_id=0, has_side_effects=True
        ),
    )(*operands)


def body(mesh, incident, material, contrast, w_first, w_middle, w_last, z_kernel, spectral):
    shapes_fit = (
        incident.shape == (2, 16, 4, 128)
        and mesh.shape["gx"] == 32
        and mesh.shape["gy"] == 1
        and w_middle.shape[0] == 32
    )
    args = (incident, material, contrast, w_first, w_middle, w_last, z_kernel, spectral)
    return fused(mesh, *args) if shapes_fit else per_device(*args)


def solution(mesh):
    placed = (
        P("grp", None, "gx", "gy"),
        P("grp", "gx", "gy"),
        P("grp", None),
        P(),
        P(),
        P(),
        P("grp", None, None),
        P("grp", "gx", None),
    )
    return jax.shard_map(
        functools.partial(body, mesh),
        mesh=mesh,
        in_specs=placed,
        out_specs=P("grp", None, "gx", "gy"),
        check_vma=False,
    )
```

```python
import functools
import math

import jax
import jax.numpy as jnp
import ml_dtypes
import numpy as np
from jax import lax
from jax.experimental import pallas as pl
from jax.experimental.pallas import tpu as pltpu
from jax.sharding import PartitionSpec as P


def padded_2(x, sides, width):
    for axis, dim in sides:
        count, length = (lax.axis_size(axis), x.shape[dim])
        up = [(i, (i + 1) % count) for i in range(count)]
        down = [(j, i) for i, j in up]
        last = lax.slice_in_dim(x, length - width, length, axis=dim)
        leading = lax.slice_in_dim(x, 0, width, axis=dim)
        before = lax.ppermute(last, axis, up)
        after = lax.ppermute(leading, axis, down)
        x = jnp.concatenate([before, x, after], axis=dim)
    return x


def conv_layer(values, weights):
    return lax.conv_general_dilated(
        values[None],
        weights,
        (1, 1, 1),
        ((1, 1), (0, 0), (0, 0)),
        dimension_numbers=("NCDHW", "OIDHW", "NCDHW"),
        preferred_element_type=jnp.float32,
    )[0]


def activate(values):
    return jax.nn.gelu(values, approximate=False).astype(jnp.bfloat16)


def dft_tables(length):
    positions = jnp.arange(length, dtype=jnp.int32)
    product = positions[:, None] * positions[None, :] % length
    angle = product.astype(jnp.float32) * (2.0 * math.pi / length)
    return (jnp.cos(angle), jnp.sin(angle))


def green_apply(source, z_kernel, spectral):
    high = lax.Precision.HIGHEST
    kr, ki = (z_kernel[0], z_kernel[1])
    lre = jnp.einsum("zw,wxy->zxy", kr, source[0], precision=high) - jnp.einsum(
        "zw,wxy->zxy", ki, source[1], precision=high
    )
    lim = jnp.einsum("zw,wxy->zxy", kr, source[1], precision=high) + jnp.einsum(
        "zw,wxy->zxy", ki, source[0], precision=high
    )
    columns = lax.all_to_all(jnp.stack([lre, lim]), "gy", split_axis=1, concat_axis=3, tiled=True)
    count_y = columns.shape[3]
    cos_y, sin_y = dft_tables(count_y)
    fwd_re = jnp.dot(columns[0], cos_y, precision=high) + jnp.dot(columns[1], sin_y, precision=high)
    fwd_im = jnp.dot(columns[1], cos_y, precision=high) - jnp.dot(columns[0], sin_y, precision=high)
    count_x = columns.shape[2] * lax.axis_size("gx")
    cos_x, sin_x = dft_tables(count_x)
    piece = lax.all_to_all(
        jnp.stack([fwd_re, fwd_im]), "gx", split_axis=3, concat_axis=2, tiled=True
    )
    ar = jnp.einsum("zxk,xq->zkq", piece[0], cos_x, precision=high) + jnp.einsum(
        "zxk,xq->zkq", piece[1], sin_x, precision=high
    )
    ai = jnp.einsum("zxk,xq->zkq", piece[1], cos_x, precision=high) - jnp.einsum(
        "zxk,xq->zkq", piece[0], sin_x, precision=high
    )
    br = spectral[0] * ar - spectral[1] * ai
    bi = spectral[0] * ai + spectral[1] * ar
    gr = jnp.einsum("zkq,qx->zxk", br, cos_x, precision=high) - jnp.einsum(
        "zkq,qx->zxk", bi, sin_x, precision=high
    )
    gi = jnp.einsum("zkq,qx->zxk", bi, cos_x, precision=high) + jnp.einsum(
        "zkq,qx->zxk", br, sin_x, precision=high
    )
    spread = jnp.stack([gr, gi]) / count_x
    rows = lax.all_to_all(spread, "gx", split_axis=2, concat_axis=3, tiled=True)
    inv_re = jnp.dot(rows[0], cos_y, precision=high) - jnp.dot(rows[1], sin_y, precision=high)
    inv_im = jnp.dot(rows[1], cos_y, precision=high) + jnp.dot(rows[0], sin_y, precision=high)
    scattered = jnp.stack([inv_re, inv_im]) / count_y
    return lax.all_to_all(scattered, "gy", split_axis=3, concat_axis=1, tiled=True)


def per_device(incident, material, contrast, w_first, w_middle, w_last, z_kernel, spectral):
    high = lax.Precision.HIGHEST
    classes = contrast.shape[0]
    selector = (material[None] == jnp.arange(classes, dtype=jnp.int32)[:, None, None, None]).astype(
        jnp.float32
    )
    chi_re = jnp.einsum("k,kzxy->zxy", contrast[:, 0], selector, precision=high)
    chi_im = jnp.einsum("k,kzxy->zxy", contrast[:, 1], selector, precision=high)
    field = incident
    pol_re = chi_re * field[0] - chi_im * field[1]
    pol_im = chi_re * field[1] + chi_im * field[0]
    features = jnp.stack([field[0], field[1], pol_re, pol_im]).astype(jnp.bfloat16)
    padded = padded_2(features, (("gx", 2), ("gy", 3)), 3)
    hidden = activate(conv_layer(padded, w_first))
    hidden = activate(conv_layer(hidden, w_middle))
    correction = conv_layer(hidden, w_last)
    source = jnp.stack([pol_re, pol_im]) + correction
    field = incident + green_apply(source, z_kernel, spectral)
    return field


def table_arrays(length, local):
    position = np.arange(length)
    angle = (position[:, None] * position[None, :] % length) * (2.0 * np.pi / length)
    cos, sin = np.cos(angle), np.sin(angle)
    order = position.reshape(length // local, local).T.reshape(-1)
    full = np.stack(
        [
            np.concatenate([cos, sin], axis=1),
            np.concatenate([cos[:, order], sin[:, order]], axis=1),
        ]
    ).astype(np.float32)
    high = full.astype(ml_dtypes.bfloat16)
    low = (full - high.astype(np.float32)).astype(ml_dtypes.bfloat16)
    return np.concatenate([high, low])


def split(x):
    high = x.astype(jnp.bfloat16)
    return high, (x - high.astype(jnp.float32)).astype(jnp.bfloat16)


def mxu(a, b):
    return jnp.dot(a, b, preferred_element_type=jnp.float32)


def dot3(a_high, a_low, b):
    b_high, b_low = split(b)
    return mxu(a_high, b_high) + (mxu(a_high, b_low) + mxu(a_low, b_high))


def gelu(x):
    return 0.5 * x * (1.0 + lax.erf(x * math.sqrt(0.5)))


def whole_kernel(
    dims,
    incident_hbm,
    material_hbm,
    contrast_hbm,
    w1_hbm,
    w2_hbm,
    w3_hbm,
    zk_hbm,
    spectral_hbm,
    tables_hbm,
    out_ref,
    incident_ref,
    material_ref,
    contrast_ref,
    w1_ref,
    w2_ref,
    w3_ref,
    zk_ref,
    spectral_ref,
    tables_ref,
    load_sem,
    base1,
    base2,
    base3,
    wt1,
    wt2,
    wt3,
    own,
    halo_left,
    halo_right,
    pol,
    feat,
    h1,
    h2,
    o3,
    scale,
    send_a,
    recv_a,
    send_b,
    recv_b,
    halo_send,
    halo_recv,
    a_send,
    a_recv,
    b_send,
    b_recv,
):
    n, nz, nx, ny, hid, classes = dims
    bf16, f32 = jnp.bfloat16, jnp.float32
    me = lax.axis_index("gx")
    right, left = lax.rem(me + 1, n), lax.rem(me + n - 1, n)
    mesh_id = pl.DeviceIdType.MESH

    pairs = (
        (incident_hbm, incident_ref),
        (material_hbm, material_ref),
        (contrast_hbm, contrast_ref),
        (w1_hbm, w1_ref),
        (w2_hbm, w2_ref),
        (w3_hbm, w3_ref),
        (zk_hbm, zk_ref),
        (spectral_hbm, spectral_ref),
        (tables_hbm, tables_ref),
    )
    loads = [
        pltpu.make_async_copy(src, dst, load_sem.at[k]) for k, (src, dst) in enumerate(pairs)
    ]
    for load in loads:
        load.start()

    barrier = pltpu.get_barrier_semaphore()

    def greet(k, carry):
        pl.semaphore_signal(
            barrier, inc=1, device_id={"gx": lax.rem(me + k, n)}, device_id_type=mesh_id
        )
        return carry

    lax.fori_loop(1, n, greet, 0, unroll=True)

    for load in loads[:3]:
        load.wait()

    for x in range(nx):
        f0 = incident_ref[0, :, x, :]
        f1 = incident_ref[1, :, x, :]
        mat = material_ref[:, x, :]
        cr = jnp.zeros_like(f0)
        ci = jnp.zeros_like(f0)
        for k in range(classes):
            hit = mat == k
            cr = jnp.where(hit, contrast_ref[0:1, k : k + 1], cr)
            ci = jnp.where(hit, contrast_ref[1:2, k : k + 1], ci)
        pr = cr * f0 - ci * f1
        pi = cr * f1 + ci * f0
        pol[0, x] = pr
        pol[1, x] = pi
        own[x] = jnp.concatenate([f0, f1, pr, pi], axis=0).astype(bf16)

    pl.semaphore_wait(barrier, n - 1)

    to_right = pltpu.make_async_remote_copy(
        src_ref=own.at[pl.ds(nx - 3, 3)],
        dst_ref=halo_left,
        send_sem=halo_send.at[0],
        recv_sem=halo_recv.at[0],
        device_id={"gx": right},
        device_id_type=mesh_id,
    )
    to_left = pltpu.make_async_remote_copy(
        src_ref=own.at[pl.ds(0, 3)],
        dst_ref=halo_right,
        send_sem=halo_send.at[1],
        recv_sem=halo_recv.at[1],
        device_id={"gx": left},
        device_id_type=mesh_id,
    )
    to_right.start()
    to_left.start()

    for load in loads[3:]:
        load.wait()
    base1[...] = jnp.zeros_like(base1)
    base2[...] = jnp.zeros_like(base2)
    base3[...] = jnp.zeros_like(base3)
    for a in range(3):
        for t in range(9):
            base1[t, :, a, 0:hid] = w1_ref[a * 9 + t].astype(f32)
            base2[t, :, hid * a : hid * a + hid] = w2_ref[a * 9 + t].astype(f32)
            b, d = divmod(t, 3)
            base3[b, 2 * d : 2 * d + 2, hid * a : hid * a + hid] = w3_ref[a * 9 + t].astype(f32)

    wide = jnp.transpose(base1[...].reshape(640, 128))[0:hid]
    lane = lax.broadcasted_iota(jnp.int32, wide.shape, 1) % nz
    for z in range(nz):
        block = wide if z == 1 else pltpu.roll(wide, (z - 1) % 640, 1)
        if z == 0:
            block = jnp.where(lane == nz - 1, 0.0, block)
        if z == nz - 1:
            block = jnp.where(lane == 0, 0.0, block)
        wt1[z * hid : z * hid + hid, :] = block.astype(bf16)
    for t in range(9):
        narrow = base2[t]
        for z in range(6):
            block = narrow if z == 0 else pltpu.roll(narrow, hid * z, 1)
            wt2[z * hid : z * hid + hid, t * 256 : t * 256 + 256] = block.astype(bf16)
    lane3 = lax.broadcasted_iota(jnp.int32, (8, 512), 1)
    for b in range(3):
        line = base3[b]
        rows = []
        for z in range(nz):
            block = line if z == 1 else pltpu.roll(line, (hid * (z - 1)) % 512, 1)
            if z == 0:
                block = jnp.where(lane3 >= 512 - hid, 0.0, block)
            if z == nz - 1:
                block = jnp.where(lane3 < hid, 0.0, block)
            rows.append(block)
        wt3[:, b * 512 : b * 512 + 512] = jnp.concatenate(rows, axis=0).astype(bf16)

    h1[:, :, 0:hid, :] = jnp.zeros((3, nx + 4, hid, ny), bf16)
    h1[:, :, (nz + 1) * hid :, :] = jnp.zeros((3, nx + 4, 3 * hid, ny), bf16)

    def shifted(x):
        return pltpu.roll(x, 1, 1), x, pltpu.roll(x, ny - 1, 1)

    def pair(ref, d, x, rows):
        return jnp.concatenate([ref[d, x, rows, :], ref[d, x + 1, rows, :]], axis=1)

    def place(x, piece):
        for d, moved in enumerate(shifted(piece.astype(f32))):
            feat[d, x] = moved.astype(bf16)

    def first(x, other):
        parts = [
            jnp.concatenate([feat[d, x + b], feat[d, other + b]], axis=1)
            for b in range(3)
            for d in range(3)
        ]
        hidden = gelu(mxu(wt1[...], jnp.concatenate(parts + [parts[0]], axis=0)))
        for half, cell in enumerate((x, other)):
            for d, moved in enumerate(shifted(hidden[:, half * ny : half * ny + ny])):
                h1[d, cell, hid : (nz + 1) * hid, :] = moved.astype(bf16)

    for x in range(nx):
        place(x + 3, own[x])
    first(3, 4)
    weights = [
        jnp.transpose(
            jnp.concatenate(
                [
                    jnp.broadcast_to(spectral_ref[part, q : q + 1, :], (2 * nz, 128))
                    for q in range(4)
                ],
                axis=0,
            )
        )
        for part in range(2)
    ]
    for part in range(2):
        scale[part] = weights[part]

    to_right.wait()
    to_left.wait()

    for x in range(3):
        place(x, halo_left[x])
        place(x + nx + 3, halo_right[x])

    def outer(i, carry):
        first(2 - i, 5 + i)
        return carry

    lax.fori_loop(0, 3, outer, 0, unroll=True)

    def second(i, carry):
        x = 2 * (i // 3)
        start = pl.multiple_of((i % 3) * (6 * hid), 64)
        rows = pl.ds(start, 8 * hid)
        parts = [pair(h1, d, x + b, rows) for b in range(3) for d in range(3)]
        hidden = gelu(mxu(wt2[...], jnp.concatenate(parts, axis=0))).astype(bf16)
        for half in range(2):
            h2[x + half, pl.ds(start, 6 * hid), :] = hidden[:, half * ny : half * ny + ny]
        return carry

    lax.fori_loop(0, 3 * ((nx + 2) // 2), second, 0, unroll=True)

    for x in range(0, nx, 2):
        parts = [
            jnp.concatenate([h2[x + b, 0 : nz * hid, :], h2[x + b + 1, 0 : nz * hid, :]], axis=1)
            for b in range(3)
        ]
        taps = mxu(wt3[...], jnp.concatenate(parts, axis=0))
        for half in range(2):
            o3[x + half] = taps[:, half * ny : half * ny + ny].reshape(nz, 8, ny)

    sources = []
    for part in range(2):
        cells = []
        for x in range(nx):
            cells.append(
                pol[part, x]
                + (
                    pltpu.roll(o3[x, :, part, :], 1, 1)
                    + o3[x, :, 2 + part, :]
                    + pltpu.roll(o3[x, :, 4 + part, :], ny - 1, 1)
                )
            )
        sources.append(jnp.concatenate(cells, axis=1))
    zk_high, zk_low = split(zk_ref[...])
    both = [dot3(zk_high, zk_low, s) for s in sources]
    lre = both[0][0:nz] - both[1][nz:]
    lim = both[1][0:nz] + both[0][nz:]
    lifted = []
    for x in range(nx):
        lifted.append(lre[:, x * ny : x * ny + ny])
        lifted.append(lim[:, x * ny : x * ny + ny])
    lifted = jnp.transpose(jnp.concatenate(lifted, axis=0))

    lane = lax.broadcasted_iota(jnp.int32, (128, 128), 1)
    real = (lane // nz) % 2 == 0
    group = lax.broadcasted_iota(jnp.int32, (n, 128), 1) // (2 * nz)

    def swap(x):
        return jnp.where(real, pltpu.roll(x, 128 - nz, 1), -pltpu.roll(x, nz, 1))

    def transform(index, x, other):
        return dot3(tables_ref[index], tables_ref[index + 2], jnp.concatenate([x, other], axis=0))

    def regroup(ref):
        slabs = [ref[:, k, :] for k in range(4)]
        blocks = []
        for g in range(4):
            block = slabs[0] if g == 0 else pltpu.roll(slabs[0], (-32 * g) % 128, 1)
            for k in range(1, 4):
                moved = slabs[k] if k == g else pltpu.roll(slabs[k], (32 * (k - g)) % 128, 1)
                block = jnp.where(group == k, moved, block)
            blocks.append(block)
        return jnp.concatenate(blocks, axis=0)

    def exchange(value, send, recv, send_sem, recv_sem):
        for j in range(n):
            send[j] = value[4 * j : 4 * j + 4, :]
        recv[pl.ds(me, 1)] = send[pl.ds(me, 1)]

        def start(k, carry):
            target = lax.rem(me + k, n)
            pltpu.make_async_remote_copy(
                src_ref=send.at[target],
                dst_ref=recv.at[me],
                send_sem=send_sem,
                recv_sem=recv_sem,
                device_id={"gx": target},
                device_id_type=mesh_id,
            ).start()
            return carry

        lax.fori_loop(1, n, start, 0, unroll=True)
        wait_all(recv, recv_sem)

    def wait_all(ref, sem):
        pltpu.make_async_copy(ref.at[pl.ds(0, n - 1)], ref.at[pl.ds(0, n - 1)], sem).wait()

    exchange(transform(0, lifted, swap(lifted)), send_a, recv_a, a_send, a_recv)

    columns = regroup(recv_a)
    spectrum = transform(1, columns, swap(columns))
    scaled = scale[0] * spectrum - scale[1] * swap(spectrum)
    exchange(transform(0, scaled, -swap(scaled)), send_b, recv_b, b_send, b_recv)

    rows = regroup(recv_b)
    result = jnp.transpose(transform(1, rows, -swap(rows))) * (1.0 / (128 * 128))
    for x in range(nx):
        for part in range(2):
            first_row = (2 * x + part) * nz
            out_ref[part, :, x, :] = (
                incident_ref[part, :, x, :] + result[first_row : first_row + nz, :]
            )
    wait_all(send_a, a_send)
    wait_all(send_b, b_send)


def fused(mesh, incident, material, contrast, w_first, w_middle, w_last, z_kernel, spectral):
    n = mesh.shape["gx"]
    _, nz, nx, ny = incident.shape
    hid = w_middle.shape[0]
    f32, bf16 = jnp.float32, jnp.bfloat16
    w1 = jnp.transpose(w_first, (2, 3, 4, 1, 0)).reshape(27, 4, hid)
    w2 = jnp.transpose(w_middle, (2, 3, 4, 0, 1)).reshape(27, hid, hid)
    w3 = jnp.transpose(w_last, (2, 3, 4, 0, 1)).reshape(27, 2, hid)
    vmem = pl.BlockSpec(memory_space=pltpu.VMEM)
    hbm = pl.BlockSpec(memory_space=pltpu.HBM)
    dims = (n, nz, nx, ny, hid, contrast.shape[0])
    dma = pltpu.SemaphoreType.DMA
    operands = (
        incident,
        material,
        contrast.T,
        w1,
        w2,
        w3,
        z_kernel.reshape(2 * nz, nz),
        spectral,
        jnp.asarray(table_arrays(128, nx)),
    )
    return pl.pallas_call(
        functools.partial(whole_kernel, dims),
        out_shape=jax.ShapeDtypeStruct(incident.shape, f32),
        in_specs=[hbm] * len(operands),
        out_specs=vmem,
        scratch_shapes=[pltpu.VMEM(x.shape, x.dtype) for x in operands]
        + [
            dma((len(operands),)),
            pltpu.VMEM((10, 4, 16, 128), f32),
            pltpu.VMEM((9, hid, 256), f32),
            pltpu.VMEM((3, 8, 512), f32),
            pltpu.VMEM((nz * hid, 640), bf16),
            pltpu.VMEM((6 * hid, 9 * 256), bf16),
            pltpu.VMEM((nz * 8, 3 * 512), bf16),
            pltpu.VMEM((nx, 4 * nz, ny), bf16),
            pltpu.VMEM((3, 4 * nz, ny), bf16),
            pltpu.VMEM((3, 4 * nz, ny), bf16),
            pltpu.VMEM((2, nx, nz, ny), f32),
            pltpu.VMEM((3, nx + 6, 4 * nz, ny), bf16),
            pltpu.VMEM((3, nx + 4, (nz + 4) * hid, ny), bf16),
            pltpu.VMEM((nx + 2, (nz + 2) * hid, ny), bf16),
            pltpu.VMEM((nx, nz, 8, ny), f32),
            pltpu.VMEM((2, 128, 128), f32),
            pltpu.VMEM((n, 4, 128), f32),
            pltpu.VMEM((n, 4, 128), f32),
            pltpu.VMEM((n, 4, 128), f32),
            pltpu.VMEM((n, 4, 128), f32),
            dma((2,)),
            dma((2,)),
            dma,
            dma,
            dma,
            dma,
        ],
        compiler_params=pltpu.CompilerParams(
            collective_id=0, has_side_effects=True, vmem_limit_bytes=40 << 20
        ),
    )(*[pltpu.with_memory_space_constraint(x, pltpu.HBM) for x in operands])


def body(mesh, incident, material, contrast, w_first, w_middle, w_last, z_kernel, spectral):
    shapes_fit = (
        incident.shape == (2, 16, 4, 128)
        and mesh.shape["gx"] == 32
        and mesh.shape["gy"] == 1
        and w_middle.shape[0] == 32
    )
    args = (incident, material, contrast, w_first, w_middle, w_last, z_kernel, spectral)
    return fused(mesh, *args) if shapes_fit else per_device(*args)


def solution(mesh):
    placed = (
        P("grp", None, "gx", "gy"),
        P("grp", "gx", "gy"),
        P("grp", None),
        P(),
        P(),
        P(),
        P("grp", None, None),
        P("grp", "gx", None),
    )
    return jax.shard_map(
        functools.partial(body, mesh),
        mesh=mesh,
        in_specs=placed,
        out_specs=P("grp", None, "gx", "gy"),
        check_vma=False,
    )
```
